128 devices in a mesh: row: 16 (over z, x_hi, core), col: 8 (over y, x_lo).
Axes of the slice: x: 4 (x_hi: 2, x_lo: 2; x = x_hi * 2 + x_lo), y: 4, z: 4, core: 2. Of those that a mesh axis runs over, the one named last changes fastest.
Arguments:
- momentum_shards: bfloat16 [6656, 18432], P(('row', 'col')), may hold values from -0.078125 to 0.078125
- shard_starts: int32 [128], replicated, may hold values from 0 to 3568, as said below
Outputs:
- update_shards: bfloat16 [6656, 18432], P(('row', 'col'))
The draws below stay inside these ranges and needn't reach their ends.
Inputs may be any that keep to these rules, and one draw needn't show every extreme that they name: `shard_starts`: starts never fall and the first is 0; shard d starts within 12 rows of d * 28, and the last one exactly 12 rows after it. Every shard has at most 52 rows and some shard has exactly 52; the 8 shards of one index of row hold at most 248 rows together, and on some index exactly 248.
All inputs are finite; a program needn't handle non-finite values.
Results may differ from the reference program's by a relative error of at most 0.02.
Values may be sent and summed in bfloat16 or wider, within the bound.
A program may use at most 128 MiB of HBM per device.

```python
import math
import jax
import jax.numpy as jnp
from jax import lax

M = 3584
N = 18432
SHARDS = 128
GROUP = 8
BASE = 28
JIT = 12
CAP = 52


def draw_shard_starts(key, part):
    shard_index = jnp.arange(SHARDS, dtype=jnp.int32)
    jitter = jax.random.randint(jax.random.fold_in(key, 11), (SHARDS,), -JIT, JIT + 1, dtype=jnp.int32)
    chosen = jax.random.randint(jax.random.fold_in(key, 12), (), 1, SHARDS // GROUP - 1, dtype=jnp.int32)
    run_start = chosen * GROUP
    jitter = jnp.where(shard_index == run_start, -JIT, jitter)
    jitter = jnp.where(shard_index == run_start + 1, JIT, jitter)
    jitter = jnp.where(shard_index == run_start + GROUP, JIT, jitter)
    jitter = jnp.where(shard_index == SHARDS - 1, JIT, jitter)
    jitter = jnp.where(shard_index == 0, 0, jitter)
    return (shard_index * BASE + jitter).astype(jnp.int32)


def block_levels(rng, dims, pieces, smallest, top_value):
    def one(dim, parts):
        steps = jax.random.uniform(jax.random.fold_in(jax.random.fold_in(rng, 6), dim), (parts,), jnp.float32, smallest / len(pieces), top_value / len(pieces))
        return jnp.repeat(jnp.exp(steps), dims[dim] // parts).reshape((-1,) + (1,) * (len(dims) - dim - 1))

    loudness = one(*pieces[0])
    for cut in pieces[1:]:
        loudness = loudness * one(*cut)
    return loudness


def normal_values(rng, extent, scale, reach, shards=(), kind=jnp.bfloat16):
    array = jax.random.normal(rng, extent, jnp.float32) * scale
    if len(shards) > 0:
        array = block_levels(rng, extent, shards, -0.22, 0.18) * array
    return jnp.clip(array, min=-reach, max=reach).astype(kind)


def setup_inputs(seed: int = 0) -> dict:
    streams_of = jax.random.split(jax.random.key(seed), 3)
    return {
        "momentum_shards": normal_values(streams_of[0], (SHARDS * CAP, N), (1.0 / (M ** 0.5 + N ** 0.5 + 6)), 0.078125, ((0, 128),)),
        "shard_starts": draw_shard_starts(jax.random.fold_in(streams_of[2], 71), 0),
    }


coef_one = 3.4445
coef_two = -4.775
coef_three = 2.0315

def reference(momentum_shards, shard_starts):
    row_ids = jnp.arange(M, dtype=jnp.int32)
    owner_shard = (lax.optimization_barrier(jnp.sum((shard_starts[None, :] <= row_ids[:, None]).astype(jnp.int32), axis=1)) - 1).astype(jnp.int32)
    source = (owner_shard * CAP + row_ids - jnp.take(shard_starts, owner_shard)).astype(jnp.int32)
    matrix = jnp.take(momentum_shards, source, axis=0)
    gram_matrix = jnp.dot(matrix, matrix.T, preferred_element_type=jnp.float32).astype(jnp.bfloat16)
    square = jnp.dot(gram_matrix, gram_matrix, preferred_element_type=jnp.float32)
    poly_matrix = (coef_two * gram_matrix.astype(jnp.float32) + coef_three * square).astype(jnp.bfloat16)
    mixed_part = jnp.dot(poly_matrix, matrix, preferred_element_type=jnp.float32)
    scaled = (math.sqrt(N) * (coef_one * matrix.astype(jnp.float32) + mixed_part)).astype(jnp.bfloat16)
    shard_ends = jnp.concatenate([shard_starts[1:], jnp.full((1,), M, jnp.int32)])
    slot_index = jnp.arange(SHARDS * CAP, dtype=jnp.int32)
    shard_ids = (slot_index // CAP).astype(jnp.int32)
    offset = (slot_index % CAP).astype(jnp.int32)
    shard_length = jnp.take(shard_ends - shard_starts, shard_ids)
    is_valid = offset < shard_length
    target = jnp.clip(jnp.take(shard_starts, shard_ids) + offset, 0, M - 1).astype(jnp.int32)
    picked_rows = jnp.take(scaled, target, axis=0)
    return jnp.where(is_valid[:, None], picked_rows, jnp.zeros_like(picked_rows))
```

```python
import math

import jax
import jax.numpy as jnp
from jax import lax
from jax.experimental import pallas as pl
from jax.experimental.pallas import tpu as pltpu
from jax.sharding import PartitionSpec as P

M = 3584
N = 18432
SHARDS = 128
CAP = 52
SLOT = 64
GROUPS = 8
MEMBERS = 16
WIN = 480
HALF = WIN // 2
PIECE = N // MEMBERS
WA = 640
WB = PIECE - WA
SLOTS = MEMBERS * SLOT
MESH = pl.DeviceIdType.MESH

coef_one = 3.4445
coef_two = -4.775
coef_three = 2.0315

GATHER = 23
ID_IN_A = 0
ID_IN_B = 16
ID_OUT_A = 32
ID_OUT_B = 48
ID_X = 64
ID_GL = ID_X + GATHER
ID_GR = ID_GL + GATHER
ID_P = ID_GR + GATHER
ID_MATE = ID_P + GATHER
ID_RS = ID_MATE + 8
ID_GRM = ID_RS + 8
ID_PM = ID_GRM + 8
IDS = ID_PM + 8

STEP_RING = (0, 3, 1, 0, 2, 3, 1, 2)
STEP_PAIR = (0, 0, 0, 1, 0, 1, 1, 1)


def pick(values, index):
    out = jnp.int32(values[0])
    for i, value in enumerate(values):
        if i and value != values[0]:
            out = jnp.where(index == i, jnp.int32(value), out)
    return out


def dot_nt(a, b):
    return lax.dot_general(a, b, (((1,), (1,)), ((), ())), preferred_element_type=jnp.float32)


def dot_nn(a, b):
    return lax.dot_general(a, b, (((1,), (0,)), ((), ())), preferred_element_type=jnp.float32)


class Gather:
    def __init__(self, net, base, ring, pair, ref, dev):
        self.net, self.base, self.ring, self.pair, self.ref, self.dev = net, base, ring, pair, ref, dev

    def at(self, part, half, step, other):
        return self.ref(part, half, (self.ring + step) % 4, (self.pair + other) % 2)

    def to(self, step, other):
        return self.dev((self.ring + step) % 4, (self.pair + other) % 2)

    def send(self, i, part, half, step, other, dest):
        ref = self.at(part, half, step, other)
        self.net.push(ref, ref, self.base + i, self.to(*dest))

    def wait(self, i, part, half, step, other):
        self.net.arrived(self.at(part, half, step, other), self.base + i)

    def ring_sends(self, part, s):
        base = 13 if part else 1 + s * 4
        for direction, half in ((0, 0), (1, 1), (0, 1), (1, 0)):
            self.send(base + direction * 2 + half, part, half, 0, s, (1 - 2 * direction, 0))

    def start_a(self):
        self.send(0, 0, None, 0, 0, (0, 1))
        self.ring_sends(0, 0)

    def start_b(self):
        self.ring_sends(1, 0)
        self.send(19, 1, None, 0, 0, (0, 1))

    def on_pair_a(self):
        self.wait(0, 0, None, 0, 1)
        self.ring_sends(0, 1)

    def on_ring(self, part, s):
        base = 13 if part else 1 + s * 4
        fwd = 17 if part else 9 + s * 2
        self.wait(base, part, 0, -1, s)
        self.send(fwd, part, 0, -1, s, (1, 0))
        self.wait(base + 3, part, 1, 1, s)
        self.send(fwd + 1, part, 1, 1, s, (-1, 0))
        self.wait(base + 1, part, 1, -1, s)
        self.wait(base + 2, part, 0, 1, s)
        if part:
            self.send(20, 1, None, -1, 0, (0, 1))
            self.send(21, 1, None, 1, 0, (0, 1))

    def on_far(self, part, s):
        fwd = 17 if part else 9 + s * 2
        self.wait(fwd, part, 0, 2, s)
        self.wait(fwd + 1, part, 1, 2, s)
        if part:
            self.send(22, 1, None, 2, 0, (0, 1))

    def on_pair_b(self, j):
        self.wait(19 + j, 1, None, (0, -1, 1, 2)[j], 1)

    def before(self, t):
        if t == 1:
            self.on_ring(0, 0)
            self.on_ring(1, 0)
            self.on_pair_a()
        elif t == 3:
            self.on_pair_b(0)
        elif t == 4:
            self.on_far(0, 0)
            self.on_far(1, 0)
        elif t == 5:
            self.on_ring(0, 1)
            self.on_pair_b(1)
        elif t == 6:
            self.on_pair_b(2)
        elif t == 7:
            self.on_far(0, 1)
            self.on_pair_b(3)

    def drain(self):
        for i, part, half in (
            [(0, 0, None)]
            + [(1 + n, 0, n % 2) for n in range(8)]
            + [(9 + n, 0, n % 2) for n in range(4)]
            + [(13 + n, 1, n % 2) for n in range(4)]
            + [(17 + n, 1, n % 2) for n in range(2)]
            + [(19 + n, 1, None) for n in range(4)]
        ):
            self.net.sent(self.at(part, half, 0, 0), self.base + i)


class Net:
    def __init__(self, send, recv, me):
        self.send, self.recv, self.me = send, recv, me

    def copy(self, src, dst, i, dev):
        return pltpu.make_async_remote_copy(
            src_ref=src, dst_ref=dst, send_sem=self.send.at[i], recv_sem=self.recv.at[i], device_id=dev, device_id_type=MESH
        )

    def push(self, src, dst, i, dev):
        self.copy(src, dst, i, dev).start()

    def arrived(self, dst, i):
        self.copy(dst, dst, i, self.me).wait_recv()

    def sent(self, src, i):
        self.copy(src, src, i, self.me).wait_send()


def kernel(
    starts, shard, out, ra, rb, fa, fb, pack, unpack, xa, xb, gown, gsnd, gmate, rsnd, rrcv, rsum, gl, gr, pb, acc, sq, sa, sb, send, recv, local
):
    row, col = lax.axis_index("row"), lax.axis_index("col")
    z, h, c = row // 4, (row // 2) % 2, row % 2
    y, q = col // 2, (col % 2 + (row // 2) % 2) % 2
    grp, k, pos = row // 2, y * 2 + q, c * 8 + col

    def device(z_, h_, c_, y_, q_):
        return ((z_ * 2 + h_) * 2 + c_, y_ * 2 + (q_ + h_) % 2)

    def member(p):
        c_, col_ = p // 8, p % 8
        return (grp * 2 + c_, col_), ((col_ // 2) * 2 + (col_ % 2 + h) % 2) * 2 + c_

    mate = device(z, h, 1 - c, y, q)
    net = Net(send, recv, mate)

    fa[...] = jnp.zeros_like(fa)
    fb[...] = jnp.zeros_like(fb)

    barrier = pltpu.get_barrier_semaphore()

    def greet(j, carry):
        dev, _ = member((pos + j) % MEMBERS)
        pl.semaphore_signal(barrier, inc=1, device_id=dev, device_id_type=MESH)
        return carry

    lax.fori_loop(1, MEMBERS, greet, 0)
    for dev in (device((z + 1) % 4, h, c, y, q), device((z + 3) % 4, h, c, y, q), device(z, 1 - h, c, y, q)):
        pl.semaphore_signal(barrier, inc=1, device_id=dev, device_id_type=MESH)
    pl.semaphore_wait(barrier, MEMBERS + 2)

    def columns(piece, off, width):
        return pl.ds(pl.multiple_of(piece * PIECE + off, 128), width)

    own = []
    for buf, base, off, width, n in ((ra, ID_IN_A, 0, WA, 0), (rb, ID_IN_B, WA, WB, 1)):

        def scatter(j, carry, buf=buf, base=base, off=off, width=width):
            dev, piece = member((pos + j) % MEMBERS)
            net.push(shard.at[:, columns(piece, off, width)], buf.at[pos], base + j, dev)
            return carry

        lax.fori_loop(1, MEMBERS, scatter, 0)
        keep = pltpu.make_async_copy(shard.at[:, columns(k * 2 + c, off, width)], buf.at[pos], local.at[n])
        keep.start()
        own.append(keep)

    first = starts[grp * MEMBERS]
    for s in range(MEMBERS):
        d = grp * MEMBERS + s
        begin = starts[d] - first
        following = starts[jnp.minimum(d + 1, SHARDS - 1)]
        length = jnp.where(d == SHARDS - 1, M, following) - starts[d]
        slot = lax.broadcasted_iota(jnp.int32, (SLOT, WIN), 0)
        place = lax.broadcasted_iota(jnp.int32, (SLOT, WIN), 1)
        hit = (place == slot + begin) & (slot < length)
        unpack[s * SLOT : (s + 1) * SLOT, :] = jnp.where(hit, 1.0, 0.0).astype(jnp.bfloat16)
    for s in range(0, MEMBERS, 2):
        lane = lax.broadcasted_iota(jnp.int32, (WIN, 2 * SLOT), 1)
        place = lax.broadcasted_iota(jnp.int32, (WIN, 2 * SLOT), 0)
        begins, lengths = [], []
        for d in (grp * MEMBERS + s, grp * MEMBERS + s + 1):
            following = starts[jnp.minimum(d + 1, SHARDS - 1)]
            begins.append(starts[d] - first)
            lengths.append(jnp.where(d == SHARDS - 1, M, following) - starts[d])
        upper = lane >= SLOT
        slot = jnp.where(upper, lane - SLOT, lane)
        begin = jnp.where(upper, begins[1], begins[0])
        length = jnp.where(upper, lengths[1], lengths[0])
        hit = (place == slot + begin) & (slot < length)
        pack[:, s * SLOT : (s + 2) * SLOT] = jnp.where(hit, 1.0, 0.0).astype(jnp.bfloat16)

    def x_ref(part, half, ring, pair):
        buf, slot = (xb if part else xa), ring * 2 + pair
        return buf.at[slot] if half is None else buf.at[slot, pl.ds(half * HALF, HALF)]

    gx = Gather(net, ID_X, z, h, x_ref, lambda ring, pair: device(ring, pair, c, y, q))

    for buf, flat, dst, base, width, n, start in ((ra, fa, xa, ID_IN_A, WA, 0, gx.start_a), (rb, fb, xb, ID_IN_B, WB, 1, gx.start_b)):
        own[n].wait()

        def landed(j, carry, buf=buf, base=base):
            net.arrived(buf.at[(pos + MEMBERS - j) % MEMBERS], base + j)
            return carry

        lax.fori_loop(1, MEMBERS, landed, 0)

        def lay(s, carry, buf=buf, flat=flat):
            flat[pl.ds(pl.multiple_of(s * SLOT, SLOT), CAP), :] = buf[s]
            return carry

        lax.fori_loop(0, MEMBERS, lay, 0)
        for lo in range(0, width, 256):
            hi = min(lo + 256, width)
            dst[grp, :, lo:hi] = dot_nn(pack[...], flat[:, lo:hi]).astype(jnp.bfloat16)
        start()

    def block_of(t):
        return ((z + pick(STEP_RING, t)) % 4) * 2 + (h + pick(STEP_PAIR, t)) % 2

    def gram(a, hh):
        rows = pl.ds(pl.multiple_of(hh * HALF, 16), HALF)
        return dot_nt(xa[grp], xa[a, rows]) + dot_nt(xb[grp], xb[a, rows])

    def finish(t):
        a = block_of(t)
        net.arrived(gmate.at[t], ID_MATE + t)
        total = gown[t % 2] + gmate[t].astype(jnp.float32)

        @pl.when(a == k)
        def _():
            rsum[...] = total

        @pl.when(a != k)
        def _():
            rsnd[t] = total.astype(jnp.bfloat16)
            j = (a + 8 - k) % 8
            net.push(rsnd.at[t], rrcv.at[j], ID_RS + j, device(z, h, c, a // 2, a % 2))

    def gram_step(t, carry):
        for i in range(1, 8):
            if i != 2:

                @pl.when(t == i)
                def _(i=i):
                    gx.before(i)

        a = block_of(t)
        gsnd[t] = gram(a, 1 - c).astype(jnp.bfloat16)
        net.push(gsnd.at[t], gmate.at[t], ID_MATE + t, mate)
        gown[t % 2] = gram(a, c)

        @pl.when(t > 0)
        def _():
            finish(t - 1)

        return carry

    lax.fori_loop(0, 8, gram_step, 0)
    finish(7)

    def collect(j, carry):
        net.arrived(rrcv.at[j], ID_RS + j)
        rsum[...] += rrcv[j].astype(jnp.float32)
        return carry

    lax.fori_loop(1, 8, collect, 0)

    g_cuts = {(0, None): (0, 272), (0, 0): (0, 144), (0, 1): (144, 128), (1, None): (272, 208), (1, 0): (272, 112), (1, 1): (384, 96)}

    def gl_ref(part, half, ring, pair):
        lo, n = g_cuts[part, half]
        return gl.at[ring * 2 + pair, pl.ds(lo, n)]

    def halves_ref(buf):
        def ref(part, half, ring, pair):
            lo, n = g_cuts[part, half]
            return buf.at[ring * 2 + pair, c, pl.ds(lo, n)]

        return ref

    over_rows = Gather(net, ID_GL, z, h, gl_ref, lambda ring, pair: device(ring, pair, c, y, q))
    over_cols = Gather(net, ID_GR, y, q, halves_ref(gr), lambda ring, pair: device(z, h, c, ring, pair))

    def column_of(t):
        return ((y + pick(STEP_RING, t)) % 4) * 2 + (q + pick(STEP_PAIR, t)) % 2

    def to_mate(buf, t, base):
        ref = buf.at[column_of(t), c]
        net.push(ref, ref, base + t, mate)

    def from_mate(buf, t, base):
        net.arrived(buf.at[column_of(t), 1 - c], base + t)

    mine = rsum[...].astype(jnp.bfloat16)
    gl[grp] = mine
    gr[k, c] = mine
    over_rows.start_a()
    over_cols.start_a()
    over_rows.start_b()
    over_cols.start_b()
    to_mate(gr, 0, ID_GRM)
    for t in range(1, 8):
        over_rows.before(t)
        over_cols.before(t)
        to_mate(gr, t, ID_GRM)
    for t in range(8):
        from_mate(gr, t, ID_GRM)

    sq[...] = jnp.zeros_like(sq)

    def square(m, carry):
        sq[...] += dot_nn(gr[m, 0], gl[m, 0:HALF]) + dot_nn(gr[m, 1], gl[m, HALF:WIN])
        return carry

    lax.fori_loop(0, 8, square, 0)
    pb[k, c] = (coef_two * gl[grp].astype(jnp.float32) + coef_three * sq[...]).astype(jnp.bfloat16)

    poly = Gather(net, ID_P, y, q, halves_ref(pb), lambda ring, pair: device(z, h, c, ring, pair))
    poly.start_a()
    poly.start_b()
    acc[...] = jnp.zeros_like(acc)

    def product(t, carry):
        for i in range(1, 8):
            if i != 2:

                @pl.when(t == i)
                def _(i=i):
                    poly.before(i)

        to_mate(pb, t, ID_PM)
        from_mate(pb, t, ID_PM)
        m = column_of(t)
        for lo, hi, buf, off in ((0, WA, xa, 0), (WA, PIECE, xb, WA)):
            acc[:, lo:hi] += dot_nn(pb[m, 0], buf[m, 0:HALF, :]) + dot_nn(pb[m, 1], buf[m, HALF:WIN, :])
        return carry

    lax.fori_loop(0, 8, product, 0)

    for src, stage, base, off, width, n in ((xa, sa, ID_OUT_A, 0, WA, 0), (xb, sb, ID_OUT_B, WA, WB, 1)):
        for lo in range(0, width, 256):
            hi = min(lo + 256, width)
            update = math.sqrt(N) * (coef_one * src[grp, :, lo:hi].astype(jnp.float32) + acc[:, off + lo : off + hi])
            rows = dot_nn(unpack[...], update.astype(jnp.bfloat16)).astype(jnp.bfloat16)
            for s in range(MEMBERS):
                stage[s, :, lo:hi] = rows[s * SLOT : s * SLOT + CAP]

        def give_back(j, carry, stage=stage, base=base, off=off, width=width):
            p = (pos + j) % MEMBERS
            dev, _ = member(p)
            net.push(stage.at[p], out.at[:, columns(k * 2 + c, off, width)], base + j, dev)
            return carry

        lax.fori_loop(1, MEMBERS, give_back, 0)
        keep = pltpu.make_async_copy(stage.at[pos], out.at[:, columns(k * 2 + c, off, width)], local.at[n])
        keep.start()
        own[n] = keep

    for base, off, width, n, buf in ((ID_OUT_A, 0, WA, 0, ra), (ID_OUT_B, WA, WB, 1, rb)):
        own[n].wait()

        def returned(j, carry, base=base, off=off, width=width):
            _, piece = member((pos + MEMBERS - j) % MEMBERS)
            net.arrived(out.at[:, columns(piece, off, width)], base + j)
            return carry

        lax.fori_loop(1, MEMBERS, returned, 0)

    for base, buf in ((ID_IN_A, ra), (ID_IN_B, rb), (ID_OUT_A, ra), (ID_OUT_B, rb)):

        def left(j, carry, base=base, buf=buf):
            net.sent(buf.at[0], base + j)
            return carry

        lax.fori_loop(1, MEMBERS, left, 0)
    for gather in (gx, over_rows, over_cols, poly):
        gather.drain()

    def left_blocks(t, carry):
        for base in (ID_MATE, ID_GRM, ID_PM):
            net.sent(gsnd.at[0], base + t)

        @pl.when(t > 0)
        def _():
            net.sent(gsnd.at[0], ID_RS + t)

        return carry

    lax.fori_loop(0, 8, left_blocks, 0)


def body(momentum_shards, shard_starts):
    bf16, f32 = jnp.bfloat16, jnp.float32
    vmem = pltpu.VMEM
    return pl.pallas_call(
        kernel,
        out_shape=jax.ShapeDtypeStruct((CAP, N), bf16),
        in_specs=[pl.BlockSpec(memory_space=pltpu.SMEM), pl.BlockSpec(memory_space=pl.ANY)],
        out_specs=pl.BlockSpec(memory_space=pl.ANY),
        scratch_shapes=[
            vmem((MEMBERS, CAP, WA), bf16),
            vmem((MEMBERS, CAP, WB), bf16),
            vmem((SLOTS, WA), bf16),
            vmem((SLOTS, WB), bf16),
            vmem((WIN, SLOTS), bf16),
            vmem((SLOTS, WIN), bf16),
            vmem((GROUPS, WIN, WA), bf16),
            vmem((GROUPS, WIN, WB), bf16),
            vmem((2, WIN, HALF), f32),
            vmem((8, WIN, HALF), bf16),
            vmem((8, WIN, HALF), bf16),
            vmem((8, WIN, HALF), bf16),
            vmem((8, WIN, HALF), bf16),
            vmem((WIN, HALF), f32),
            vmem((8, WIN, HALF), bf16),
            vmem((8, 2, WIN, HALF), bf16),
            vmem((8, 2, WIN, HALF), bf16),
            vmem((WIN, PIECE), f32),
            vmem((WIN, HALF), f32),
            vmem((MEMBERS, CAP, WA), bf16),
            vmem((MEMBERS, CAP, WB), bf16),
            pltpu.SemaphoreType.DMA((IDS,)),
            pltpu.SemaphoreType.DMA((IDS,)),
            pltpu.SemaphoreType.DMA((2,)),
        ],
        compiler_params=pltpu.CompilerParams(collective_id=0, has_side_effects=True, vmem_limit_bytes=62 * 1024 * 1024),
    )(shard_starts, momentum_shards)


def solution(mesh):
    in_specs = (P(("row", "col"), None), P())
    out_specs = P(("row", "col"), None)
    return jax.shard_map(body, mesh=mesh, in_specs=in_specs, out_specs=out_specs, check_vma=False)
```
